32 devices in a mesh: group: 4 (over z), blk: 8 (over y, x, core).
Axes of the slice: x: 2, y: 2, z: 4, core: 2. Of those that a mesh axis runs over, the one named last changes fastest.
Arguments:
- cotangent: bfloat16 [24576, 3584], P(('group', 'blk')), may hold values from -6 to 6
- pre_act: bfloat16 [24576, 2, 1024], P(('group', 'blk')), may hold values from -6 to 6
- down_weight: bfloat16 [1024, 2, 3584], P('blk'), may hold values from -0.09375 to 0.09375
- tile_expert: int32 [192], P(('group', 'blk')), may hold values from 0 to 1
- tile_fill: int32 [192], P(('group', 'blk')), may hold values from 1 to 128, as said below
Outputs:
- act_grad: bfloat16 [24576, 2, 1024], P(('group', 'blk'))
- weight_grad: float32 [1024, 2, 3584], P(('group', 'blk'))
The draws below stay inside these ranges and needn't reach their ends.
Inputs may be any that keep to these rules, and one draw needn't show every extreme that they name: tile_fill reaches 128 in every draw.
All inputs are finite; a program needn't handle non-finite values.
Results may differ from the reference program's by a relative error of at most 0.0029.
Values may be sent and summed in bfloat16 or wider, within the bound.
No kernel may reach another device: no remote copies, remote signals or barrier semaphores. Data moves between devices by JAX's collectives and lax.ppermute only.
A program may use at most 192 MiB of HBM per device.

```python
import jax
import jax.numpy as jnp
from jax import lax

D = 3584
H = 1024
EXPERTS = 2
TILE = 128
TILES = 6
TILES_ALL = 192
ROWS_ALL = 24576
N_GROUP = 4
N_BLK = 8


def draw_tile_fill(key, part):
    fill_values = jax.random.randint(key, (TILES_ALL,), 1, TILE + 1)
    return fill_values.at[0].set(TILE).astype(jnp.int32)


def plant(entries, rng, smallest, top_value):
    dims = entries.shape
    spot = [jax.random.randint(jax.random.fold_in(rng, axis), (), 0, dims[axis]) for axis in range(len(dims))]
    entries = entries.at[tuple(spot)].set(smallest)
    longest = dims.index(max(dims))
    spot[longest] = (spot[longest] + 1) % dims[longest]
    return entries.at[tuple(spot)].set(top_value)


def with_spikes(array, rng, source, target, shards_of, factor):
    owner, partner = [(jnp.arange(array.shape[dim]) // (array.shape[dim] // shards_of)).reshape([-1 if axis == dim else 1 for axis in range(array.ndim)]) for dim in (source, target)]
    chosen = jax.random.permutation(rng, shards_of)[partner]
    strong = (owner == chosen) | (owner == (partner + shards_of // 2) % shards_of)
    return jnp.where(strong, factor * array, array)


def steps_of(own_key, extent, cuts, smallest, largest):
    factor_of = 1.0
    for position, blocks in cuts:
        steps = jax.random.uniform(jax.random.fold_in(jax.random.fold_in(own_key, 6), position), (blocks,), jnp.float32, smallest / len(cuts), largest / len(cuts))
        factor_of = factor_of * jnp.repeat(jnp.exp(steps), extent[position] // blocks).reshape((-1,) + (1,) * (len(extent) - 1 - position))
    return factor_of


def normal_values(key, dims, scale, reach, pieces=(), held_as=jnp.bfloat16):
    factor_of = steps_of(key, dims, pieces, -0.22, 0.18) if pieces else 1.0
    result = jax.random.normal(key, dims, jnp.float32) * scale * factor_of
    return jnp.minimum(jnp.maximum(result, -reach), reach).astype(held_as)


def gaussian_with(stream_key, dims, spread, reach, cuts, heavy, kind=jnp.bfloat16):
    values = spread * jax.random.normal(stream_key, dims, jnp.float32)
    if cuts:
        values = values * steps_of(stream_key, dims, cuts, -0.22, 0.18)
    return jnp.clip(with_spikes(values, jax.random.fold_in(stream_key, 3), *heavy), -reach, reach).astype(kind)


def setup_inputs(seed: int = 0) -> dict:
    streams_of = jax.random.split(jax.random.key(seed), 6)
    cotangent = gaussian_with(streams_of[0], (ROWS_ALL, D), 1.0, 6.0, ((0, 32),), (0, 1, 32, 2.75))
    pre_act = normal_values(streams_of[1], (ROWS_ALL, 2, H), 1.5, 6.0, ((0, 32),))
    down_weight = normal_values(streams_of[2], (H, EXPERTS, D), D ** -0.5, 0.09375, ((0, 8),))
    tile_expert = plant(jax.random.randint(streams_of[3], (TILES_ALL,), 0, EXPERTS), jax.random.fold_in(streams_of[3], 1), 0, EXPERTS - 1).astype(jnp.int32)
    tile_fill = draw_tile_fill(jax.random.fold_in(streams_of[5], 71), 0)
    return {"cotangent": cotangent, "pre_act": pre_act, "down_weight": down_weight, "tile_expert": tile_expert, "tile_fill": tile_fill}


grad_factor = 0.015625


def reference(cotangent, pre_act, down_weight, tile_expert, tile_fill):
    device_count = N_GROUP * N_BLK
    cot_all = cotangent.reshape(device_count, TILES, TILE, D)
    pre_all = pre_act.reshape(device_count, TILES, TILE, 2, H)
    expert_all = tile_expert.reshape(device_count, TILES)
    fill_all = tile_fill.reshape(device_count, TILES)

    def one_device(total, item):
        cot_tiles, pre_tiles, expert_ids, fill_values = item
        chosen = jnp.take(down_weight, expert_ids, axis=1).astype(jnp.float32)
        hidden_grad = jnp.einsum("trd,htd->trh", cot_tiles.astype(jnp.float32), chosen)
        live_rows = (jnp.arange(TILE, dtype=jnp.int32)[None, :] < fill_values[:, None]).astype(jnp.float32)[:, :, None]
        gate_pre = pre_tiles[:, :, 0, :].astype(jnp.float32)
        up_pre = pre_tiles[:, :, 1, :].astype(jnp.float32)
        sigmoid_gate = jax.nn.sigmoid(gate_pre)
        silu_gate = gate_pre * sigmoid_gate
        activation = (live_rows * silu_gate * up_pre).astype(jnp.bfloat16)
        gate_grad = live_rows * hidden_grad * up_pre * sigmoid_gate * (1.0 + gate_pre * (1.0 - sigmoid_gate))
        up_grad = live_rows * hidden_grad * silu_gate
        grads = jnp.stack([gate_grad, up_grad], axis=2).astype(jnp.bfloat16)
        per_tile = jnp.einsum("trh,trd->thd", activation.astype(jnp.float32), cot_tiles.astype(jnp.float32))
        expert_hot = (expert_ids[:, None] == jnp.arange(EXPERTS, dtype=jnp.int32)[None, :]).astype(jnp.float32)
        term = jnp.einsum("te,thd->hed", expert_hot, per_tile)
        return total + term, grads

    start_total = jnp.zeros((H, EXPERTS, D), jnp.float32)
    total, grads = lax.scan(one_device, start_total, (cot_all, pre_all, expert_all, fill_all))
    return grads.reshape(ROWS_ALL, 2, H), total * grad_factor
```

```python
import functools

import jax
import jax.numpy as jnp
from jax import lax
from jax.experimental import pallas as pl
from jax.experimental.pallas import tpu as pltpu
from jax.sharding import PartitionSpec as P


grad_factor = 0.015625
MIB = 1024 * 1024


def bits_of(size):
    return [1 << i for i in range(size.bit_length() - 1)]


def flip(value, axis, size, mask):
    return lax.ppermute(value, axis, [(i, i ^ mask) for i in range(size)])


def params(mib):
    return pltpu.CompilerParams(vmem_limit_bytes=mib * MIB)


def cost(flops, size):
    return pl.CostEstimate(flops=flops, bytes_accessed=size, transcendentals=0)


def gate_terms(pre_ref, fill):
    pre = jnp.swapaxes(pre_ref[...], 0, 1)
    gate, up = pre[0].astype(jnp.float32), pre[1].astype(jnp.float32)
    position = lax.broadcasted_iota(jnp.int32, (gate.shape[0], 1), 0)
    live = (position < fill).astype(jnp.float32)
    sig = 1.0 / (1.0 + jnp.exp(-gate))
    return live, gate, up, sig


def activation_kernel(fill_ref, pre_ref, out_ref):
    live, gate, up, sig = gate_terms(pre_ref, fill_ref[pl.program_id(0)])
    out_ref[...] = (live * (gate * sig) * up).T.astype(out_ref.dtype)


def activation_t(tile_fill, pre_act):
    tiles = tile_fill.shape[0]
    rows, two, hidden = pre_act.shape
    tile = rows // tiles
    return pl.pallas_call(
        activation_kernel,
        grid_spec=pltpu.PrefetchScalarGridSpec(
            num_scalar_prefetch=1,
            grid=(tiles,),
            in_specs=[pl.BlockSpec((tile, two, hidden), lambda t, f: (t, 0, 0))],
            out_specs=pl.BlockSpec((hidden, tile), lambda t, f: (0, t)),
        ),
        out_shape=jax.ShapeDtypeStruct((hidden, rows), pre_act.dtype),
        compiler_params=params(58),
        cost_estimate=cost(0, 6 * rows * hidden),
        name="activation_t",
    )(tile_fill, pre_act)


def part_rows(core_ref, mine, rows, granules, move):
    def blocks(granule):
        for j in range(rows // (2 * granule)):
            keep = pl.multiple_of((2 * j + mine) * granule, granule)
            send = pl.multiple_of((2 * j + 1 - mine) * granule, granule)
            move(pl.ds(j * granule, granule), pl.ds(keep, granule), pl.ds(send, granule))

    if granules[0] == granules[1]:
        blocks(granules[0])
    else:
        for core in range(2):
            pl.when(core_ref == core)(functools.partial(blocks, granules[core]))


def term_kernel(granules, first, count, tiles, ids_ref, pos_ref, own_ref, other_ref, cot_ref, cot2_ref, send, keep, acc):
    tile = own_ref.shape[1] // tiles

    def masked(act_ref, start, e):
        parts = []
        for t in range(tiles):
            part = act_ref[:, t * tile : (t + 1) * tile]
            parts.append(jnp.where(ids_ref[start + t] == e, part, jnp.zeros_like(part)))
        return jnp.concatenate(parts, axis=1)

    for e in range(send.shape[0]):
        acc[...] = jnp.dot(
            masked(own_ref, 0, e), cot_ref[:, first : first + count], preferred_element_type=jnp.float32
        ) + jnp.dot(
            masked(other_ref, tiles, e), cot2_ref[:, first : first + count], preferred_element_type=jnp.float32
        )

        def move(to, kept, sent):
            keep[e, to, :] = acc[kept, :]
            send[e, to, :] = acc[sent, :].astype(send.dtype)

        part_rows(pos_ref[0], pos_ref[1], acc.shape[0], granules, move)


def terms(ids, pos, own_t, other_t, cot, cot2, granules, experts, first, count, block):
    hidden, rows = own_t.shape
    half = cot.shape[1] // 2
    tiles = ids.shape[0] // 2
    return pl.pallas_call(
        functools.partial(term_kernel, granules, first, count, tiles),
        grid_spec=pltpu.PrefetchScalarGridSpec(
            num_scalar_prefetch=2,
            grid=(hidden // block,),
            in_specs=[
                pl.BlockSpec((block, rows), lambda g, i, p: (g, 0)),
                pl.BlockSpec((block, rows), lambda g, i, p: (g, 0)),
                pl.BlockSpec((rows, half), lambda g, i, p: (0, p[0])),
                pl.BlockSpec((rows, half), lambda g, i, p: (0, p[0])),
            ],
            out_specs=[pl.BlockSpec((experts, block // 2, count), lambda g, i, p: (0, g, 0))] * 2,
            scratch_shapes=[pltpu.VMEM((block, count), jnp.float32)],
        ),
        out_shape=[
            jax.ShapeDtypeStruct((experts, hidden // 2, count), jnp.bfloat16),
            jax.ShapeDtypeStruct((experts, hidden // 2, count), jnp.float32),
        ],
        compiler_params=params(58),
        cost_estimate=cost(4 * hidden * 2 * rows * count, 12 * hidden * count + 8 * rows * half),
        name="terms",
    )(ids, pos, own_t, other_t, cot, cot2)


def step_kernel(granules, step, pos_ref, keep_ref, recv_ref, *refs):
    send, keep, acc = refs[-3:]
    for e in range(keep_ref.shape[0]):
        acc[...] = keep_ref[e] + recv_ref[e].astype(jnp.float32)

        def move(to, kept, sent):
            keep[e, to, :] = acc[kept, :]
            send[e, to, :] = acc[sent, :].astype(send.dtype)

        part_rows(pos_ref[0], pos_ref[step], acc.shape[0], granules, move)


def halve(pos, step, keep, recv, granules, kind, after=()):
    experts, rows, count = keep.shape
    return pl.pallas_call(
        functools.partial(step_kernel, granules, step),
        in_specs=[pl.BlockSpec(memory_space=pltpu.SMEM)]
        + [pl.BlockSpec(memory_space=pltpu.VMEM)] * 2
        + [pl.BlockSpec(memory_space=pl.ANY)] * len(after),
        out_specs=[pl.BlockSpec(memory_space=pltpu.VMEM)] * 2,
        scratch_shapes=[pltpu.VMEM((rows, count), jnp.float32)],
        out_shape=[
            jax.ShapeDtypeStruct((experts, rows // 2, count), kind),
            jax.ShapeDtypeStruct((experts, rows // 2, count), jnp.float32),
        ],
        compiler_params=params(16),
        cost_estimate=cost(0, 9 * experts * rows * count),
        name="halve",
    )(pos, keep, recv, *after)


def finish_kernel(firsts, core_ref, *refs):
    out = refs[-1]
    keeps, others = refs[: len(firsts)], refs[len(firsts) : -1]
    half = out.shape[2] // 2
    for core in range(2):

        @pl.when(core_ref[0] == core)
        def _():
            for first, keep, other in zip(firsts, keeps, others):
                count = keep.shape[2]
                for e in range(out.shape[1]):
                    start = core * half + first
                    out[:, e, start : start + count] = keep[e] * grad_factor
                    start = (1 - core) * half + first
                    out[:, e, start : start + count] = other[e] * grad_factor


def finish(core, firsts, keeps, others, shape):
    return pl.pallas_call(
        functools.partial(finish_kernel, firsts),
        in_specs=[pl.BlockSpec(memory_space=pltpu.SMEM)] + [pl.BlockSpec(memory_space=pltpu.VMEM)] * (2 * len(firsts)),
        out_specs=pl.BlockSpec(memory_space=pltpu.VMEM),
        out_shape=jax.ShapeDtypeStruct(shape, jnp.float32),
        compiler_params=params(16),
        name="finish",
    )(core, *keeps, *others)


def grad_kernel(units, ids_ref, fill_ref, col_ref, slot_ref, cot_ref, pre_ref, *refs):
    parts = refs[: 2 * units]
    out_ref, raw, weight, grad, sems = refs[-5:]
    s, j = pl.program_id(0), pl.program_id(1)
    rows = parts[0].shape[0]
    wide = 2 * rows
    tile = cot_ref.shape[0] // 2

    def copy(i):
        to = pl.ds(pl.multiple_of(slot_ref[i] * rows, rows), rows)
        return pltpu.make_async_copy(parts[i], raw.at[i // 2, to], sems.at[i])

    @pl.when((s == 0) & (j == 0))
    def _():
        for i in range(2 * units):
            copy(i).start()
        for i in range(2 * units):
            copy(i).wait()
            if i % 2:
                u = i // 2
                weight[:, u * wide : (u + 1) * wide, :] = jnp.swapaxes(raw[u], 0, 1)

    @pl.when(j == 0)
    def _():
        first, second = ids_ref[2 * s], ids_ref[2 * s + 1]

        def product(e):
            full = lax.dot_general(
                cot_ref[...], weight[e], (((1,), (1,)), ((), ())), preferred_element_type=jnp.float32
            )
            return [full[:, i * wide : (i + 1) * wide] for i in range(units)]

        @pl.when(first == second)
        def _():
            for i, part in enumerate(product(first)):
                grad[i] = part

        @pl.when(first != second)
        def _():
            for n, e in enumerate((first, second)):
                for i, part in enumerate(product(e)):
                    grad[i, n * tile : (n + 1) * tile, :] = part[n * tile : (n + 1) * tile]

    for n in range(2):
        of = pl.ds(n * tile, tile)
        live, gate, up, sig = gate_terms(pre_ref.at[of], fill_ref[2 * s + n])
        base = live * grad[j, of, :]
        both = jnp.stack([base * up * sig * (1.0 + gate * (1.0 - sig)), base * (gate * sig)])
        out_ref[of, :, :] = jnp.swapaxes(both.astype(out_ref.dtype), 0, 1)


def input_grads(ids, fill, cols, slots, cot, pre_act, parts, into=None):
    tiles = ids.shape[0]
    rows, width = cot.shape
    pair = 2 * rows // tiles
    two = pre_act.shape[1]
    own, experts, _ = parts[0].shape
    units = len(parts) // 2
    columns = pl.BlockSpec((pair, two, 2 * own), lambda t, j, i, f, c, sl: (t, 0, c[j]))
    anywhere = pl.BlockSpec(memory_space=pl.ANY)
    extra = () if into is None else (into,)
    work = rows * own * units
    return pl.pallas_call(
        functools.partial(grad_kernel, units),
        grid_spec=pltpu.PrefetchScalarGridSpec(
            num_scalar_prefetch=4,
            grid=(tiles // 2, units),
            in_specs=[pl.BlockSpec((pair, width), lambda t, *_: (t, 0)), columns]
            + [anywhere] * (len(parts) + len(extra)),
            out_specs=columns,
            scratch_shapes=[
                pltpu.VMEM((units, 2 * own, experts, width), cot.dtype),
                pltpu.VMEM((experts, units * 2 * own, width), cot.dtype),
                pltpu.VMEM((units, pair, 2 * own), jnp.float32),
                pltpu.SemaphoreType.DMA((len(parts),)),
            ],
        ),
        out_shape=jax.ShapeDtypeStruct(pre_act.shape, pre_act.dtype),
        input_output_aliases={} if into is None else {6 + len(parts): 0},
        compiler_params=params(58),
        cost_estimate=cost(4 * work * width, 2 * (rows * width + 4 * experts * own * units * width + 16 * work)),
        name="input_grads",
    )(ids, fill, cols, slots, cot, pre_act, *parts, *extra)


def body(splits, cotangent, pre_act, down_weight, tile_expert, tile_fill):
    groups, blks = lax.axis_size("group"), lax.axis_size("blk")
    group, blk = lax.axis_index("group"), lax.axis_index("blk")
    hidden = pre_act.shape[2]
    experts, width = down_weight.shape[1:]
    half = width // 2
    owned = hidden // (groups * blks)
    upper = bits_of(blks)[1:]
    zbits = bits_of(groups)
    core = blk & 1
    orders = [upper, upper[::-1]]

    def by_core(pair):
        return jnp.where(core == 0, pair[0], pair[1])

    def across(value, step):
        return lax.ppermute(value, "blk", [(i, i ^ orders[i & 1][step]) for i in range(blks)])

    def swap(value):
        return flip(value, "blk", blks, 1)

    cot2 = swap(cotangent)

    if len(upper) == 2 and groups > 1:
        moves = []
        for g in range(groups):
            for b in range(blks):
                source = (b ^ orders[b & 1][0]) & ~1 | ((b ^ g) & 1)
                moves.append((g * blks + source, g * blks + b))
        straight = lax.ppermute(down_weight, ("group", "blk"), moves)
        round_z = flip(straight, "group", groups, 1)
        far = across(straight, 1)
        own2 = swap(down_weight)
        straight2 = swap(straight)
        round2 = swap(round_z)
        far2 = swap(far)
        near = [by_core([o[0] for o in orders]), by_core([o[1] for o in orders])]
        picked = core ^ (group & 1)
        units = [
            (down_weight, own2, 0, core),
            (straight, round_z, near[0], picked),
            (straight2, round2, near[1], 1 - picked),
            (far, far2, upper[0] ^ upper[1], picked),
        ]
    else:
        held, masks = [down_weight], ([0], [0])
        for step in range(len(upper)):
            held = held + [across(part, step) for part in held]
            masks = tuple(m + [i ^ order[step] for i in m] for m, order in zip(masks, orders))
        units = []
        for i, part in enumerate(held):
            mate = masks[1].index(masks[0][i])
            units.append((part, swap(held[mate]), by_core([m[i] for m in masks]), core))
    cols = jnp.stack([(blk ^ mask) >> 1 for _, _, mask, _ in units]).astype(jnp.int32)
    slots = jnp.stack([s for _, _, _, at in units for s in (at, 1 - at)]).astype(jnp.int32)

    act = activation_t(tile_fill, pre_act)
    act2 = swap(act)
    ids = jnp.concatenate([tile_expert, swap(tile_expert)])
    act_grad = None
    at = 0
    for size in splits:
        parts = [p for unit in units[at : at + size] for p in unit[:2]]
        act_grad = input_grads(
            tile_expert, tile_fill, cols[at : at + size], slots[2 * at : 2 * (at + size)],
            cotangent, pre_act, parts, act_grad,
        )
        at += size

    def granules(step):
        out = []
        for order in orders:
            left = [1] + order[step + 1 :]
            out.append(owned * (1 << sum(1 for m in left if m < order[step])))
        return tuple(out)

    bits = [(blk & by_core([order[step] for order in orders])) != 0 for step in range(len(upper))]
    sizes = [granules(step) for step in range(len(upper))]
    for mask in zbits:
        bits.append((group & mask) != 0)
        sizes.append((2 * owned, 2 * owned))
    bits.append(core != 0)
    sizes.append((owned, owned))
    pos = jnp.stack([core] + [bit.astype(jnp.int32) for bit in bits])

    firsts, counts = (0, half - 768), (half - 768, 768)
    sends, keeps = [], []
    for first, count in zip(firsts, counts):
        send, keep = terms(ids, pos, act, act2, cotangent, cot2, sizes[0], experts, first, count, blks * owned)
        for step in range(len(bits) - 1):
            if step < len(upper):
                recv = across(send, step)
            else:
                recv = flip(send, "group", groups, zbits[step - len(upper)])
            last = step == len(bits) - 2
            send, keep = halve(
                pos, step + 2, keep, recv, sizes[step + 1], jnp.float32 if last else jnp.bfloat16
            )
        sends.append(swap(send))
        keeps.append(keep)
    weight_grad = finish(core.reshape(1), firsts, keeps, sends, (owned, experts, width))
    return act_grad, weight_grad


def solution(mesh):
    placed = (
        P(("group", "blk"), None),
        P(("group", "blk"), None, None),
        P("blk", None, None),
        P(("group", "blk")),
        P(("group", "blk")),
    )
    shape = dict(mesh.shape)
    usual = shape["blk"] == 8 and shape["group"] == 4
    splits = (1, 2, 1) if usual else (1,) * (shape["blk"] // 2)

    def run(*args):
        return body(splits, *args)

    return jax.shard_map(
        run,
        mesh=mesh,
        in_specs=placed,
        out_specs=(P(("group", "blk"), None, None), P(("group", "blk"), None, None)),
        check_vma=False,
    )
```

```python
import functools

import jax
import jax.numpy as jnp
from jax import lax
from jax.experimental import pallas as pl
from jax.experimental.pallas import tpu as pltpu
from jax.sharding import PartitionSpec as P


grad_factor = 0.015625
MIB = 1024 * 1024


def bits_of(size):
    return [1 << i for i in range(size.bit_length() - 1)]


def flip(value, axis, size, mask):
    return lax.ppermute(value, axis, [(i, i ^ mask) for i in range(size)])


def params(mib):
    return pltpu.CompilerParams(vmem_limit_bytes=mib * MIB)


def cost(flops, size):
    return pl.CostEstimate(flops=flops, bytes_accessed=size, transcendentals=0)


def gate_terms(pre_ref, fill):
    pre = jnp.swapaxes(pre_ref[...], 0, 1)
    gate, up = pre[0].astype(jnp.float32), pre[1].astype(jnp.float32)
    position = lax.broadcasted_iota(jnp.int32, (gate.shape[0], 1), 0)
    live = (position < fill).astype(jnp.float32)
    sig = 1.0 / (1.0 + jnp.exp(-gate))
    return live, gate, up, sig


def activation_kernel(tile, fill_ref, pre_ref, out_ref):
    count = pre_ref.shape[0] // tile
    for n in range(count):
        of = pl.ds(n * tile, tile)
        live, gate, up, sig = gate_terms(pre_ref.at[of], fill_ref[count * pl.program_id(0) + n])
        out_ref[:, of] = (live * (gate * sig) * up).astype(out_ref.dtype).T


def activation_t(tile_fill, pre_act):
    tiles = tile_fill.shape[0]
    rows, two, hidden = pre_act.shape
    tile = rows // tiles
    block = 2 * tile
    return pl.pallas_call(
        functools.partial(activation_kernel, tile),
        grid_spec=pltpu.PrefetchScalarGridSpec(
            num_scalar_prefetch=1,
            grid=(rows // block,),
            in_specs=[pl.BlockSpec((block, two, hidden), lambda t, f: (t, 0, 0))],
            out_specs=pl.BlockSpec((hidden, block), lambda t, f: (0, t)),
        ),
        out_shape=jax.ShapeDtypeStruct((hidden, rows), pre_act.dtype),
        compiler_params=params(32),
        cost_estimate=cost(0, 6 * rows * hidden),
        name="activation_t",
    )(tile_fill, pre_act)


def part_rows(core_ref, mine, rows, granules, move):
    def blocks(granule):
        for j in range(rows // (2 * granule)):
            keep = pl.multiple_of((2 * j + mine) * granule, granule)
            send = pl.multiple_of((2 * j + 1 - mine) * granule, granule)
            move(pl.ds(j * granule, granule), pl.ds(keep, granule), pl.ds(send, granule))

    if granules[0] == granules[1]:
        blocks(granules[0])
    else:
        for core in range(2):
            pl.when(core_ref == core)(functools.partial(blocks, granules[core]))


def load_terms(kind, first, granules, ids_ref, pos_ref, act_hbm, cot_hbm, act, masked, cot, act_sem, cot_sem):
    hidden, rows = act.shape[1:]
    tiles = ids_ref[0].shape[0]
    tile = rows // tiles
    e = pl.program_id(0)

    def act_copy(n):
        return pltpu.make_async_copy(act_hbm[n], act.at[n], act_sem.at[n])

    def cot_copy(n):
        half = cot_hbm[n].shape[1] // 2
        columns = pl.ds(pl.multiple_of(pos_ref[0] * half + first, 128), cot.shape[1])
        return pltpu.make_async_copy(cot_hbm[n].at[:, columns], cot.at[pl.ds(n * rows, rows)], cot_sem.at[n])

    @pl.when(e == 0)
    def _():
        for n in range(2):
            act_copy(n).start()
        for n in range(2):
            cot_copy(n).start()
        for n in range(2):
            act_copy(n).wait()

    def move(to, kept, sent):
        of = kept if kind else sent
        for n in range(2):
            for t in range(tiles):
                part = act[n, of, t * tile : (t + 1) * tile]
                at = n * rows + t * tile
                masked[to, at : at + tile] = jnp.where(ids_ref[n][t] == e, part, jnp.zeros_like(part))

    part_rows(pos_ref[0], pos_ref[1], hidden, granules, move)

    @pl.when(e == 0)
    def _():
        for n in range(2):
            cot_copy(n).wait()


def sent_kernel(first, granules, ids_ref, ids2_ref, pos_ref, own_ref, other_ref, cot_ref, cot2_ref, send, *scratch):
    masked, cot = scratch[1:3]
    load_terms(0, first, granules, (ids_ref, ids2_ref), pos_ref, (own_ref, other_ref), (cot_ref, cot2_ref), *scratch)
    send[0] = jnp.dot(masked[...], cot[...], preferred_element_type=jnp.float32).astype(send.dtype)


def kept_kernel(first, granules, following, ids_ref, ids2_ref, pos_ref, own_ref, other_ref, cot_ref, cot2_ref, recv, send, keep, acc, *scratch):
    masked, cot = scratch[1:3]
    load_terms(1, first, granules, (ids_ref, ids2_ref), pos_ref, (own_ref, other_ref), (cot_ref, cot2_ref), *scratch)
    acc[...] = recv[0].astype(jnp.float32) + jnp.dot(masked[...], cot[...], preferred_element_type=jnp.float32)

    def move(to, kept, sent):
        keep[0, to, :] = acc[kept, :]
        send[0, to, :] = acc[sent, :].astype(send.dtype)

    part_rows(pos_ref[0], pos_ref[2], acc.shape[0], following, move)


def terms(kernel, sources, count, experts, recv=()):
    hidden, rows = sources[3].shape
    anywhere = pl.BlockSpec(memory_space=pl.ANY)
    dma = pltpu.SemaphoreType.DMA

    def spec(part):
        return pl.BlockSpec((1, hidden // part, count), lambda e, *_: (e, 0, 0))

    if recv:
        kinds = ((4, jnp.bfloat16), (4, jnp.float32))
    else:
        kinds = ((2, jnp.bfloat16),)
    return pl.pallas_call(
        kernel,
        grid_spec=pltpu.PrefetchScalarGridSpec(
            num_scalar_prefetch=3,
            grid=(experts,),
            in_specs=[anywhere] * 4 + [spec(2)] * len(recv),
            out_specs=[spec(part) for part, _ in kinds],
            scratch_shapes=[pltpu.VMEM((hidden // 2, count), jnp.float32)] * len(recv)
            + [
                pltpu.VMEM((2, hidden, rows), jnp.bfloat16),
                pltpu.VMEM((hidden // 2, 2 * rows), jnp.bfloat16),
                pltpu.VMEM((2 * rows, count), jnp.bfloat16),
                dma((2,)),
                dma((2,)),
            ],
        ),
        out_shape=[jax.ShapeDtypeStruct((experts, hidden // part, count), kind) for part, kind in kinds],
        compiler_params=params(32),
        cost_estimate=cost(2 * hidden * 2 * rows * count, 6 * hidden * count + 8 * rows * count),
        name="terms",
    )(*sources, *recv)


def step_kernel(granules, step, pos_ref, keep_ref, recv_ref, *refs):
    send, keep, acc = refs[-3:]
    for e in range(keep_ref.shape[0]):
        acc[...] = keep_ref[e] + recv_ref[e].astype(jnp.float32)

        def move(to, kept, sent):
            keep[e, to, :] = acc[kept, :]
            send[e, to, :] = acc[sent, :].astype(send.dtype)

        part_rows(pos_ref[0], pos_ref[step], acc.shape[0], granules, move)


def halve(pos, step, keep, recv, granules, kind, after=()):
    experts, rows, count = keep.shape
    return pl.pallas_call(
        functools.partial(step_kernel, granules, step),
        in_specs=[pl.BlockSpec(memory_space=pltpu.SMEM)]
        + [pl.BlockSpec(memory_space=pltpu.VMEM)] * 2
        + [pl.BlockSpec(memory_space=pl.ANY)] * len(after),
        out_specs=[pl.BlockSpec(memory_space=pltpu.VMEM)] * 2,
        scratch_shapes=[pltpu.VMEM((rows, count), jnp.float32)],
        out_shape=[
            jax.ShapeDtypeStruct((experts, rows // 2, count), kind),
            jax.ShapeDtypeStruct((experts, rows // 2, count), jnp.float32),
        ],
        compiler_params=params(16),
        cost_estimate=cost(0, 9 * experts * rows * count),
        name="halve",
    )(pos, keep, recv, *after)


def finish_kernel(firsts, core_ref, *refs):
    out = refs[-1]
    keeps, others = refs[: len(firsts)], refs[len(firsts) : -1]
    half = out.shape[2] // 2
    for core in range(2):

        @pl.when(core_ref[0] == core)
        def _():
            for first, keep, other in zip(firsts, keeps, others):
                count = keep.shape[2]
                for e in range(out.shape[1]):
                    start = core * half + first
                    out[:, e, start : start + count] = keep[e] * grad_factor
                    start = (1 - core) * half + first
                    out[:, e, start : start + count] = other[e] * grad_factor


def finish(core, firsts, keeps, others, shape):
    return pl.pallas_call(
        functools.partial(finish_kernel, firsts),
        in_specs=[pl.BlockSpec(memory_space=pltpu.SMEM)] + [pl.BlockSpec(memory_space=pltpu.VMEM)] * (2 * len(firsts)),
        out_specs=pl.BlockSpec(memory_space=pltpu.VMEM),
        out_shape=jax.ShapeDtypeStruct(shape, jnp.float32),
        compiler_params=params(16),
        name="finish",
    )(core, *keeps, *others)


def grad_kernel(at, units, ids_ref, fill_ref, where_ref, cot_hbm, pre_hbm, *refs):
    parts = refs[: 2 * units]
    out_hbm, raw, weight, cot, pre, out, grad, part_sem, cot_sem, pre_sem, out_sem = refs[-11:]
    rows = parts[0].shape[0]
    wide = 2 * rows
    pairs, pair = cot.shape[:2]
    tile = pair // 2

    def part_copy(i):
        to = pl.ds(pl.multiple_of(where_ref[3 * (at + i // 2) + 1 + i % 2] * rows, rows), rows)
        return pltpu.make_async_copy(parts[i], raw.at[i // 2, to], part_sem.at[i])

    def cot_copy(s):
        return pltpu.make_async_copy(cot_hbm.at[pl.ds(s * pair, pair)], cot.at[s], cot_sem.at[s])

    def columns(u):
        return pl.ds(pl.multiple_of(where_ref[3 * (at + u)] * wide, wide), wide)

    def pre_copy(u):
        return pltpu.make_async_copy(pre_hbm.at[:, :, columns(u)], pre.at[u], pre_sem.at[u])

    def out_copy(u, s):
        of = pl.ds(s * pair, pair)
        return pltpu.make_async_copy(out.at[u, of], out_hbm.at[of, :, columns(u)], out_sem.at[u, s])

    for i in range(2 * units):
        part_copy(i).start()
    for s in range(pairs):
        cot_copy(s).start()
    for u in range(units):
        pre_copy(u).start()
    for u in range(units):
        part_copy(2 * u).wait()
        part_copy(2 * u + 1).wait()
        weight[:, u * wide : (u + 1) * wide, :] = jnp.swapaxes(raw[u], 0, 1)
    for u in range(units):
        pre_copy(u).wait()

    @pl.loop(0, pairs)
    def _(s):
        cot_copy(s).wait()
        first, second = ids_ref[2 * s], ids_ref[2 * s + 1]

        def product(e):
            return lax.dot_general(cot[s], weight[e], (((1,), (1,)), ((), ())), preferred_element_type=jnp.float32)

        grad[...] = product(first)

        @pl.when(first != second)
        def _():
            grad[tile:, :] = product(second)[tile:]

        for u in range(units):
            for n in range(2):
                of = pl.ds(pl.multiple_of(s * pair + n * tile, tile), tile)
                live, gate, up, sig = gate_terms(pre.at[u, of], fill_ref[2 * s + n])
                base = live * grad[n * tile : (n + 1) * tile, u * wide : (u + 1) * wide]
                both = jnp.stack([base * up * sig * (1.0 + gate * (1.0 - sig)), base * (gate * sig)])
                out[u, of, :, :] = jnp.swapaxes(both.astype(out.dtype), 0, 1)
            out_copy(u, s).start()

    for u in range(units):
        for s in range(pairs):
            out_copy(u, s).wait()


def input_grads(ids, fill, where, at, cot, pre_act, parts, into=None):
    tiles = ids.shape[0]
    rows, width = cot.shape
    pairs = tiles // 2
    two = pre_act.shape[1]
    own, experts, _ = parts[0].shape
    units = len(parts) // 2
    anywhere = pl.BlockSpec(memory_space=pl.ANY)
    extra = () if into is None else (into,)
    work = rows * own * units
    dma = pltpu.SemaphoreType.DMA
    return pl.pallas_call(
        functools.partial(grad_kernel, at, units),
        in_specs=[pl.BlockSpec(memory_space=pltpu.SMEM)] * 3 + [anywhere] * (2 + len(parts) + len(extra)),
        out_specs=anywhere,
        scratch_shapes=[
            pltpu.VMEM((units, 2 * own, experts, width), cot.dtype),
            pltpu.VMEM((experts, units * 2 * own, width), cot.dtype),
            pltpu.VMEM((pairs, rows // pairs, width), cot.dtype),
            pltpu.VMEM((units, rows, two, 2 * own), pre_act.dtype),
            pltpu.VMEM((units, rows, two, 2 * own), pre_act.dtype),
            pltpu.VMEM((rows // pairs, units * 2 * own), jnp.float32),
            dma((len(parts),)),
            dma((pairs,)),
            dma((units,)),
            dma((units, pairs)),
        ],
        out_shape=jax.ShapeDtypeStruct(pre_act.shape, pre_act.dtype),
        input_output_aliases={} if into is None else {5 + len(parts): 0},
        compiler_params=params(32),
        cost_estimate=cost(4 * work * width, 2 * (rows * width + 4 * experts * own * units * width + 16 * work)),
        name="input_grads",
    )(ids, fill, where, cot, pre_act, *parts, *extra)


def body(splits, cotangent, pre_act, down_weight, tile_expert, tile_fill):
    groups, blks = lax.axis_size("group"), lax.axis_size("blk")
    group, blk = lax.axis_index("group"), lax.axis_index("blk")
    hidden = pre_act.shape[2]
    experts, width = down_weight.shape[1:]
    half = width // 2
    owned = hidden // (groups * blks)
    upper = bits_of(blks)[1:]
    zbits = bits_of(groups)
    core = blk & 1
    orders = [upper, upper[::-1]]

    def by_core(pair):
        return jnp.where(core == 0, pair[0], pair[1])

    def across(value, step):
        return lax.ppermute(value, "blk", [(i, i ^ orders[i & 1][step]) for i in range(blks)])

    def swap(value):
        return flip(value, "blk", blks, 1)

    cot2 = swap(cotangent)

    if len(upper) == 2 and groups > 1:
        moves = []
        for g in range(groups):
            for b in range(blks):
                source = (b ^ orders[b & 1][0]) & ~1 | ((b ^ g) & 1)
                moves.append((g * blks + source, g * blks + b))
        straight = lax.ppermute(down_weight, ("group", "blk"), moves)
        round_z = flip(straight, "group", groups, 1)
        far = across(straight, 1)
        own2 = swap(down_weight)
        straight2 = swap(straight)
        round2 = swap(round_z)
        far2 = swap(far)
        near = [by_core([o[0] for o in orders]), by_core([o[1] for o in orders])]
        picked = core ^ (group & 1)
        units = [
            (down_weight, own2, 0, core),
            (straight, round_z, near[0], picked),
            (straight2, round2, near[1], 1 - picked),
            (far, far2, upper[0] ^ upper[1], picked),
        ]
    else:
        held, masks = [down_weight], ([0], [0])
        for step in range(len(upper)):
            held = held + [across(part, step) for part in held]
            masks = tuple(m + [i ^ order[step] for i in m] for m, order in zip(masks, orders))
        units = []
        for i, part in enumerate(held):
            mate = masks[1].index(masks[0][i])
            units.append((part, swap(held[mate]), by_core([m[i] for m in masks]), core))
    where = jnp.stack([i for _, _, mask, slot in units for i in ((blk ^ mask) >> 1, slot, 1 - slot)])

    act = activation_t(tile_fill, pre_act)
    act2 = swap(act)
    ids2 = swap(tile_expert)
    act_grad = None
    at = 0
    for size in splits:
        parts = [p for unit in units[at : at + size] for p in unit[:2]]
        act_grad = input_grads(tile_expert, tile_fill, where, at, cotangent, pre_act, parts, act_grad)
        at += size

    def granules(step):
        out = []
        for order in orders:
            left = [1] + order[step + 1 :]
            out.append(owned * (1 << sum(1 for m in left if m < order[step])))
        return tuple(out)

    bits = [(blk & by_core([order[step] for order in orders])) != 0 for step in range(len(upper))]
    sizes = [granules(step) for step in range(len(upper))]
    for mask in zbits:
        bits.append((group & mask) != 0)
        sizes.append((2 * owned, 2 * owned))
    bits.append(core != 0)
    sizes.append((owned, owned))
    pos = jnp.stack([core] + [bit.astype(jnp.int32) for bit in bits])

    firsts, counts = (0, half - 768), (half - 768, 768)
    sends, keeps = [], []
    sources = (tile_expert, ids2, pos, act, act2, cotangent, cot2)
    for first, count in zip(firsts, counts):
        (send,) = terms(functools.partial(sent_kernel, first, sizes[0]), sources, count, experts)
        for step in range(len(bits) - 1):
            if step < len(upper):
                recv = across(send, step)
            else:
                recv = flip(send, "group", groups, zbits[step - len(upper)])
            if step == 0:
                kernel = functools.partial(kept_kernel, first, sizes[0], sizes[1])
                send, keep = terms(kernel, sources, count, experts, (recv,))
                continue
            last = step == len(bits) - 2
            send, keep = halve(
                pos, step + 2, keep, recv, sizes[step + 1], jnp.float32 if last else jnp.bfloat16
            )
        sends.append(swap(send))
        keeps.append(keep)
    weight_grad = finish(core.reshape(1), firsts, keeps, sends, (owned, experts, width))
    return act_grad, weight_grad


def solution(mesh):
    placed = (
        P(("group", "blk"), None),
        P(("group", "blk"), None, None),
        P("blk", None, None),
        P(("group", "blk")),
        P(("group", "blk")),
    )
    shape = dict(mesh.shape)
    usual = shape["blk"] == 8 and shape["group"] == 4
    splits = (1, 1, 1, 1) if usual else (1,) * (shape["blk"] // 2)

    def run(*args):
        return body(splits, *args)

    return jax.shard_map(
        run,
        mesh=mesh,
        in_specs=placed,
        out_specs=(P(("group", "blk"), None, None), P(("group", "blk"), None, None)),
        check_vma=False,
    )
```

```python
import functools

import jax
import jax.numpy as jnp
from jax import lax
from jax.experimental import pallas as pl
from jax.experimental.pallas import tpu as pltpu
from jax.sharding import PartitionSpec as P


grad_factor = 0.015625
MIB = 1024 * 1024


def bits_of(size):
    return [1 << i for i in range(size.bit_length() - 1)]


def flip(value, axis, size, mask):
    return lax.ppermute(value, axis, [(i, i ^ mask) for i in range(size)])


def params(mib):
    return pltpu.CompilerParams(vmem_limit_bytes=mib * MIB)


def cost(flops, size):
    return pl.CostEstimate(flops=flops, bytes_accessed=size, transcendentals=0)


def gate_terms(pre_ref, fill):
    pre = jnp.swapaxes(pre_ref[...], 0, 1)
    gate, up = pre[0].astype(jnp.float32), pre[1].astype(jnp.float32)
    position = lax.broadcasted_iota(jnp.int32, (gate.shape[0], 1), 0)
    live = (position < fill).astype(jnp.float32)
    sig = 1.0 / (1.0 + jnp.exp(-gate))
    return live, gate, up, sig


def activation_kernel(tile, fill_ref, pre_ref, out_ref):
    count = pre_ref.shape[0] // tile
    for n in range(count):
        of = pl.ds(n * tile, tile)
        live, gate, up, sig = gate_terms(pre_ref.at[of], fill_ref[count * pl.program_id(0) + n])
        out_ref[:, of] = (live * (gate * sig) * up).astype(out_ref.dtype).T


def activation_t(tile_fill, pre_act):
    tiles = tile_fill.shape[0]
    rows, two, hidden = pre_act.shape
    tile = rows // tiles
    block = 2 * tile
    return pl.pallas_call(
        functools.partial(activation_kernel, tile),
        grid_spec=pltpu.PrefetchScalarGridSpec(
            num_scalar_prefetch=1,
            grid=(rows // block,),
            in_specs=[pl.BlockSpec((block, two, hidden), lambda t, f: (t, 0, 0))],
            out_specs=pl.BlockSpec((hidden, block), lambda t, f: (0, t)),
        ),
        out_shape=jax.ShapeDtypeStruct((hidden, rows), pre_act.dtype),
        compiler_params=params(18),
        cost_estimate=cost(0, 6 * rows * hidden),
        name="activation_t",
    )(tile_fill, pre_act)


def part_rows(core_ref, mine, rows, granules, move):
    def blocks(granule):
        for j in range(rows // (2 * granule)):
            keep = pl.multiple_of((2 * j + mine) * granule, granule)
            send = pl.multiple_of((2 * j + 1 - mine) * granule, granule)
            move(pl.ds(j * granule, granule), pl.ds(keep, granule), pl.ds(send, granule))

    if granules[0] == granules[1]:
        blocks(granules[0])
    else:
        for core in range(2):
            pl.when(core_ref == core)(functools.partial(blocks, granules[core]))


def load_terms(kind, first, granules, ids_ref, pos_ref, act_hbm, cot_hbm, act, masked, cot, act_sem, cot_sem):
    hidden, rows = act.shape[1:]
    tiles = ids_ref[0].shape[0]
    tile = rows // tiles
    e = pl.program_id(0)

    def act_copy(n):
        return pltpu.make_async_copy(act_hbm[n], act.at[n], act_sem.at[n])

    def cot_copy(n):
        half = cot_hbm[n].shape[1] // 2
        columns = pl.ds(pl.multiple_of(pos_ref[0] * half + first, 128), cot.shape[1])
        return pltpu.make_async_copy(cot_hbm[n].at[:, columns], cot.at[pl.ds(n * rows, rows)], cot_sem.at[n])

    @pl.when(e == 0)
    def _():
        for n in range(2):
            act_copy(n).start()
        for n in range(2):
            cot_copy(n).start()
        for n in range(2):
            act_copy(n).wait()

    def move(to, kept, sent):
        of = kept if kind else sent
        for n in range(2):
            for t in range(tiles):
                part = act[n, of, t * tile : (t + 1) * tile]
                at = n * rows + t * tile
                masked[to, at : at + tile] = jnp.where(ids_ref[n][t] == e, part, jnp.zeros_like(part))

    part_rows(pos_ref[0], pos_ref[1], hidden, granules, move)

    @pl.when(e == 0)
    def _():
        for n in range(2):
            cot_copy(n).wait()


def sent_kernel(first, granules, ids_ref, ids2_ref, pos_ref, own_ref, other_ref, cot_ref, cot2_ref, send, *scratch):
    masked, cot = scratch[1:3]
    load_terms(0, first, granules, (ids_ref, ids2_ref), pos_ref, (own_ref, other_ref), (cot_ref, cot2_ref), *scratch)
    send[0] = jnp.dot(masked[...], cot[...], preferred_element_type=jnp.float32).astype(send.dtype)


def kept_kernel(first, granules, following, ids_ref, ids2_ref, pos_ref, own_ref, other_ref, cot_ref, cot2_ref, recv, send, keep, acc, *scratch):
    masked, cot = scratch[1:3]
    load_terms(1, first, granules, (ids_ref, ids2_ref), pos_ref, (own_ref, other_ref), (cot_ref, cot2_ref), *scratch)
    acc[...] = recv[0].astype(jnp.float32) + jnp.dot(masked[...], cot[...], preferred_element_type=jnp.float32)

    def move(to, kept, sent):
        keep[0, to, :] = acc[kept, :]
        send[0, to, :] = acc[sent, :].astype(send.dtype)

    part_rows(pos_ref[0], pos_ref[2], acc.shape[0], following, move)


def terms(kernel, sources, count, experts, recv=()):
    hidden, rows = sources[3].shape
    anywhere = pl.BlockSpec(memory_space=pl.ANY)
    dma = pltpu.SemaphoreType.DMA

    def spec(part):
        return pl.BlockSpec((1, hidden // part, count), lambda e, *_: (e, 0, 0))

    if recv:
        kinds = ((4, jnp.bfloat16), (4, jnp.float32))
    else:
        kinds = ((2, jnp.bfloat16),)
    return pl.pallas_call(
        kernel,
        grid_spec=pltpu.PrefetchScalarGridSpec(
            num_scalar_prefetch=3,
            grid=(experts,),
            in_specs=[anywhere] * 4 + [spec(2)] * len(recv),
            out_specs=[spec(part) for part, _ in kinds],
            scratch_shapes=[pltpu.VMEM((hidden // 2, count), jnp.float32)] * len(recv)
            + [
                pltpu.VMEM((2, hidden, rows), jnp.bfloat16),
                pltpu.VMEM((hidden // 2, 2 * rows), jnp.bfloat16),
                pltpu.VMEM((2 * rows, count), jnp.bfloat16),
                dma((2,)),
                dma((2,)),
            ],
        ),
        out_shape=[jax.ShapeDtypeStruct((experts, hidden // part, count), kind) for part, kind in kinds],
        compiler_params=params(18 if recv else 58),
        cost_estimate=cost(2 * hidden * 2 * rows * count, 6 * hidden * count + 8 * rows * count),
        name="terms",
    )(*sources, *recv)


def step_kernel(granules, step, pos_ref, keep_ref, recv_ref, *refs):
    send, keep, acc = refs[-3:]
    for e in range(keep_ref.shape[0]):
        acc[...] = keep_ref[e] + recv_ref[e].astype(jnp.float32)

        def move(to, kept, sent):
            keep[e, to, :] = acc[kept, :]
            send[e, to, :] = acc[sent, :].astype(send.dtype)

        part_rows(pos_ref[0], pos_ref[step], acc.shape[0], granules, move)


def halve(pos, step, keep, recv, granules, kind, after=()):
    experts, rows, count = keep.shape
    return pl.pallas_call(
        functools.partial(step_kernel, granules, step),
        in_specs=[pl.BlockSpec(memory_space=pltpu.SMEM)]
        + [pl.BlockSpec(memory_space=pltpu.VMEM)] * 2
        + [pl.BlockSpec(memory_space=pl.ANY)] * len(after),
        out_specs=[pl.BlockSpec(memory_space=pltpu.VMEM)] * 2,
        scratch_shapes=[pltpu.VMEM((rows, count), jnp.float32)],
        out_shape=[
            jax.ShapeDtypeStruct((experts, rows // 2, count), kind),
            jax.ShapeDtypeStruct((experts, rows // 2, count), jnp.float32),
        ],
        compiler_params=params(16),
        cost_estimate=cost(0, 9 * experts * rows * count),
        name="halve",
    )(pos, keep, recv, *after)


def finish_kernel(firsts, core_ref, *refs):
    out = refs[-1]
    keeps, others = refs[: len(firsts)], refs[len(firsts) : -1]
    half = out.shape[2] // 2
    for core in range(2):

        @pl.when(core_ref[0] == core)
        def _():
            for first, keep, other in zip(firsts, keeps, others):
                count = keep.shape[2]
                for e in range(out.shape[1]):
                    start = core * half + first
                    out[:, e, start : start + count] = keep[e] * grad_factor
                    start = (1 - core) * half + first
                    out[:, e, start : start + count] = other[e] * grad_factor


def finish(core, firsts, keeps, others, shape):
    return pl.pallas_call(
        functools.partial(finish_kernel, firsts),
        in_specs=[pl.BlockSpec(memory_space=pltpu.SMEM)] + [pl.BlockSpec(memory_space=pltpu.VMEM)] * (2 * len(firsts)),
        out_specs=pl.BlockSpec(memory_space=pltpu.VMEM),
        out_shape=jax.ShapeDtypeStruct(shape, jnp.float32),
        compiler_params=params(16),
        name="finish",
    )(core, *keeps, *others)


def grad_kernel(at, units, ids_ref, fill_ref, where_ref, cot, pre_hbm, *refs):
    parts = refs[: 2 * units]
    out_hbm, raw, weight, pre, out, grad, part_sem, pre_sem, out_sem = refs[-9:]
    rows = parts[0].shape[0]
    wide = 2 * rows
    tile = cot.shape[0] // ids_ref.shape[0]
    pair, pairs = 2 * tile, ids_ref.shape[0] // 2

    def part_copy(i):
        to = pl.ds(pl.multiple_of(where_ref[3 * (at + i // 2) + 1 + i % 2] * rows, rows), rows)
        return pltpu.make_async_copy(parts[i], raw.at[i // 2, to], part_sem.at[i])

    def columns(u):
        return pl.ds(pl.multiple_of(where_ref[3 * (at + u)] * wide, wide), wide)

    def pre_copy(u):
        return pltpu.make_async_copy(pre_hbm.at[:, :, columns(u)], pre.at[u], pre_sem.at[u])

    def out_copy(u, s):
        of = pl.ds(s * pair, pair)
        return pltpu.make_async_copy(out.at[u, of], out_hbm.at[of, :, columns(u)], out_sem.at[u, s])

    for i in range(2 * units):
        part_copy(i).start()
    for u in range(units):
        pre_copy(u).start()
    for u in range(units):
        part_copy(2 * u).wait()
        part_copy(2 * u + 1).wait()
        weight[:, u * wide : (u + 1) * wide, :] = jnp.swapaxes(raw[u], 0, 1)
    for u in range(units):
        pre_copy(u).wait()

    @pl.loop(0, pairs)
    def _(s):
        first, second = ids_ref[2 * s], ids_ref[2 * s + 1]

        def product(e):
            rows_of = cot[pl.ds(pl.multiple_of(s * pair, pair), pair), :]
            return lax.dot_general(rows_of, weight[e], (((1,), (1,)), ((), ())), preferred_element_type=jnp.float32)

        grad[...] = product(first)

        @pl.when(first != second)
        def _():
            grad[tile:, :] = product(second)[tile:]

        for u in range(units):
            for n in range(2):
                of = pl.ds(pl.multiple_of(s * pair + n * tile, tile), tile)
                live, gate, up, sig = gate_terms(pre.at[u, of], fill_ref[2 * s + n])
                base = live * grad[n * tile : (n + 1) * tile, u * wide : (u + 1) * wide]
                both = jnp.stack([base * up * sig * (1.0 + gate * (1.0 - sig)), base * (gate * sig)])
                out[u, of, :, :] = jnp.swapaxes(both.astype(out.dtype), 0, 1)
            out_copy(u, s).start()

    for u in range(units):
        for s in range(pairs):
            out_copy(u, s).wait()


def input_grads(ids, fill, where, at, cot, pre_act, parts, into=None):
    tiles = ids.shape[0]
    rows, width = cot.shape
    pairs = tiles // 2
    two = pre_act.shape[1]
    own, experts, _ = parts[0].shape
    units = len(parts) // 2
    anywhere = pl.BlockSpec(memory_space=pl.ANY)
    extra = () if into is None else (into,)
    work = rows * own * units
    dma = pltpu.SemaphoreType.DMA
    return pl.pallas_call(
        functools.partial(grad_kernel, at, units),
        in_specs=[pl.BlockSpec(memory_space=pltpu.SMEM)] * 3
        + [pl.BlockSpec(memory_space=pltpu.VMEM)]
        + [anywhere] * (1 + len(parts) + len(extra)),
        out_specs=anywhere,
        scratch_shapes=[
            pltpu.VMEM((units, 2 * own, experts, width), cot.dtype),
            pltpu.VMEM((experts, units * 2 * own, width), cot.dtype),
            pltpu.VMEM((units, rows, two, 2 * own), pre_act.dtype),
            pltpu.VMEM((units, rows, two, 2 * own), pre_act.dtype),
            pltpu.VMEM((rows // pairs, units * 2 * own), jnp.float32),
            dma((len(parts),)),
            dma((units,)),
            dma((units, pairs)),
        ],
        out_shape=jax.ShapeDtypeStruct(pre_act.shape, pre_act.dtype),
        input_output_aliases={} if into is None else {5 + len(parts): 0},
        compiler_params=params(18),
        cost_estimate=cost(4 * work * width, 2 * (rows * width + 4 * experts * own * units * width + 16 * work)),
        name="input_grads",
    )(ids, fill, where, cot, pre_act, *parts, *extra)


def body(splits, cotangent, pre_act, down_weight, tile_expert, tile_fill):
    groups, blks = lax.axis_size("group"), lax.axis_size("blk")
    group, blk = lax.axis_index("group"), lax.axis_index("blk")
    hidden = pre_act.shape[2]
    experts, width = down_weight.shape[1:]
    half = width // 2
    owned = hidden // (groups * blks)
    upper = bits_of(blks)[1:]
    zbits = bits_of(groups)
    core = blk & 1
    orders = [upper, upper[::-1]]

    def by_core(pair):
        return jnp.where(core == 0, pair[0], pair[1])

    def across(value, step):
        return lax.ppermute(value, "blk", [(i, i ^ orders[i & 1][step]) for i in range(blks)])

    def swap(value):
        return flip(value, "blk", blks, 1)

    cot2 = swap(cotangent)

    if len(upper) == 2 and groups > 1:
        moves = []
        for g in range(groups):
            for b in range(blks):
                source = (b ^ orders[b & 1][0]) & ~1 | ((b ^ g) & 1)
                moves.append((g * blks + source, g * blks + b))
        straight = lax.ppermute(down_weight, ("group", "blk"), moves)
        round_z = flip(straight, "group", groups, 1)
        far = across(straight, 1)
        own2 = swap(down_weight)
        straight2 = swap(straight)
        round2 = swap(round_z)
        far2 = swap(far)
        near = [by_core([o[0] for o in orders]), by_core([o[1] for o in orders])]
        picked = core ^ (group & 1)
        units = [
            (down_weight, own2, 0, core),
            (straight, round_z, near[0], picked),
            (straight2, round2, near[1], 1 - picked),
            (far, far2, upper[0] ^ upper[1], picked),
        ]
    else:
        held, masks = [down_weight], ([0], [0])
        for step in range(len(upper)):
            held = held + [across(part, step) for part in held]
            masks = tuple(m + [i ^ order[step] for i in m] for m, order in zip(masks, orders))
        units = []
        for i, part in enumerate(held):
            mate = masks[1].index(masks[0][i])
            units.append((part, swap(held[mate]), by_core([m[i] for m in masks]), core))
    where = jnp.stack([i for _, _, mask, slot in units for i in ((blk ^ mask) >> 1, slot, 1 - slot)])

    act = activation_t(tile_fill, pre_act)
    act2 = swap(act)
    ids2 = swap(tile_expert)
    act_grad = None
    at = 0
    for size in splits:
        parts = [p for unit in units[at : at + size] for p in unit[:2]]
        act_grad = input_grads(tile_expert, tile_fill, where, at, cotangent, pre_act, parts, act_grad)
        at += size

    def granules(step):
        out = []
        for order in orders:
            left = [1] + order[step + 1 :]
            out.append(owned * (1 << sum(1 for m in left if m < order[step])))
        return tuple(out)

    bits = [(blk & by_core([order[step] for order in orders])) != 0 for step in range(len(upper))]
    sizes = [granules(step) for step in range(len(upper))]
    for mask in zbits:
        bits.append((group & mask) != 0)
        sizes.append((2 * owned, 2 * owned))
    bits.append(core != 0)
    sizes.append((owned, owned))
    pos = jnp.stack([core] + [bit.astype(jnp.int32) for bit in bits])

    firsts, counts = (0, half - 768), (half - 768, 768)
    sends, keeps = [], []
    sources = (tile_expert, ids2, pos, act, act2, cotangent, cot2)
    for first, count in zip(firsts, counts):
        (send,) = terms(functools.partial(sent_kernel, first, sizes[0]), sources, count, experts)
        for step in range(len(bits) - 1):
            if step < len(upper):
                recv = across(send, step)
            else:
                recv = flip(send, "group", groups, zbits[step - len(upper)])
            if step == 0:
                kernel = functools.partial(kept_kernel, first, sizes[0], sizes[1])
                send, keep = terms(kernel, sources, count, experts, (recv,))
                continue
            last = step == len(bits) - 2
            send, keep = halve(
                pos, step + 2, keep, recv, sizes[step + 1], jnp.float32 if last else jnp.bfloat16
            )
        sends.append(swap(send))
        keeps.append(keep)
    weight_grad = finish(core.reshape(1), firsts, keeps, sends, (owned, experts, width))
    return act_grad, weight_grad


def solution(mesh):
    placed = (
        P(("group", "blk"), None),
        P(("group", "blk"), None, None),
        P("blk", None, None),
        P(("group", "blk")),
        P(("group", "blk")),
    )
    shape = dict(mesh.shape)
    usual = shape["blk"] == 8 and shape["group"] == 4
    splits = (1, 1, 1, 1) if usual else (1,) * (shape["blk"] // 2)

    def run(*args):
        return body(splits, *args)

    return jax.shard_map(
        run,
        mesh=mesh,
        in_specs=placed,
        out_specs=(P(("group", "blk"), None, None), P(("group", "blk"), None, None)),
        check_vma=False,
    )
```
